256 devices in a mesh: dp: 16 (over y_lo, x, core), ctx: 16 (over y_hi, z).
Axes of the slice: x: 4, y: 4 (y_hi: 2, y_lo: 2; y = y_hi * 2 + y_lo), z: 8, core: 2. Of those that a mesh axis runs over, the one named last changes fastest.
Arguments:
- patches: bfloat16 [262144, 1024], P(('dp', 'ctx')), parts along dimension 0, may hold values from -6 to 6
- visible_count: int32 [256], P('dp'), parts along dimension 0, may hold values from 1 to 6, 32 in all
- visible_order: int32 [256, 8], P(('dp', 'ctx')), parts along dimension 0, may hold values from 0 to 7, each once within a row
- ln_gain: float32 [1024], replicated, may hold values from 1.5 to 12
- w_qkv: bfloat16 [1024, 3072], replicated, may hold values from -0.1875 to 0.1875
- w_out: bfloat16 [1024, 1024], replicated, may hold values from -0.1875 to 0.1875
Outputs:
- mixed: bfloat16 [65536, 1024], P(('dp', 'ctx')), parts along dimension 0
The draws below stay inside these ranges and needn't reach their ends.
There are 16 independent parts, one for each index of `dp`. The reference program is written for one: setup_inputs(seed, part) draws one part's arguments, and reference() takes and returns one part's arrays. A program takes and returns all parts, laid end to end along the dimension named above; an argument that names none is the same for every part. Nothing has to cross between parts.
Inputs may be any that keep to these rules, and one draw needn't show every extreme that they name: `visible_count`: the counts sum to 32; one region has exactly 6. `visible_order`: each row is an order of the 8 blocks of its region; the first visible_count of them are visible.
All inputs are finite; a program needn't handle non-finite values.
Results may differ from the reference program's by a relative error of at most 0.005.
The reference program's roundings to bfloat16 on the way count: a program that leaves them out, or rounds other values in their place, can miss the bound.
Values may be sent and summed in bfloat16 or wider, within the bound.
No kernel may reach another device: no remote copies, remote signals or barrier semaphores. Data moves between devices by JAX's collectives and lax.ppermute only.
A program may use at most 64 MiB of HBM per device.

```python
import math
import jax
import jax.numpy as jnp
import numpy as np
from jax import lax

D = 1024
HEADS = 16
HDIM = 64
BLOCK = 128
BLK_DEV = 8
PATCHES = 16384
TOTAL_BLK = 32
MOST_BLK = 6
TOTAL_ROWS = 4096
N_CTX = 16


def draw_patches(key, part):
    first_key = jax.random.fold_in(key, 0)
    values = jax.random.normal(first_key, (PATCHES, D), jnp.float32)
    return jnp.clip(values, -6.0, 6.0).astype(jnp.bfloat16)


def draw_ln_gain(key, part):
    return jax.random.uniform(key, (D,), jnp.float32, 1.5, 2.5)


def split_up(number_of, total, most, skew):
    loads = [(1 << 20) // math.isqrt(rank ** skew) + 1 for rank in range(2, number_of + 1)]
    spare, given = total - most - (number_of - 1), [1] * (number_of - 1)
    while spare > 0:
        candidates = [i for i in range(number_of - 1) if given[i] < most]
        pool, left = sum([loads[i] for i in candidates]), spare
        for i in candidates:
            addition = min(most - given[i], max(1, left * loads[i] // pool), spare)
            given[i] = given[i] + addition
            spare = spare - addition
    return np.array([most] + given)


def uneven_parts(stream_key, amount, total, reach, slope):
    if amount == 2:
        one = jax.random.randint(stream_key, (), max(1, total - reach), min(reach, total - 1) + 1)
        return jnp.stack([one, total - one])
    tallies = jnp.asarray(split_up(amount, total, reach, slope), jnp.int32)
    twos = (amount - 1) // 2
    donor, sink = tallies[1:1 + 2 * twos:2], tallies[2:2 + 2 * twos:2]
    room = jnp.minimum(donor - 1, reach - sink)
    moved = jax.random.randint(jax.random.fold_in(stream_key, 1), (twos,), 0, 1 << 20) % (room + 1)
    tallies = tallies.at[1:1 + 2 * twos:2].set(donor - moved).at[2:2 + 2 * twos:2].set(sink + moved)
    return tallies[jax.random.permutation(jax.random.fold_in(stream_key, 2), amount)]


def normal_values(key, shape, scale, reach, kind=jnp.bfloat16):
    return jnp.clip(scale * jax.random.normal(key, shape, jnp.float32), -reach, reach).astype(kind)


def setup_inputs(seed: int = 0, part: int = 0) -> dict:
    keys = jax.random.split(jax.random.key(seed), 7)
    part_splits = jax.random.split(jax.random.fold_in(keys[6], part), 7)
    return {
        "patches": draw_patches(jax.random.fold_in(jax.random.fold_in(keys[6], part), 71), part),
        "visible_count": uneven_parts(part_splits[1], N_CTX, TOTAL_BLK, MOST_BLK, 2).astype(jnp.int32),
        "visible_order": jax.vmap(lambda own: jax.random.permutation(own, BLK_DEV))(jax.random.split(part_splits[2], N_CTX)).reshape((N_CTX, BLK_DEV)).astype(jnp.int32),
        "ln_gain": draw_ln_gain(jax.random.fold_in(keys[6], 71), part),
        "w_qkv": normal_values(keys[4], (D, 3 * D), D ** -0.5, 0.1875),
        "w_out": normal_values(keys[5], (D, D), D ** -0.5, 0.1875),
    }


epsilon = 1e-05

def layer_norm(rows_in, gain):
    values = rows_in.astype(jnp.float32)
    row_mean = lax.optimization_barrier(jnp.mean(values, axis=-1, keepdims=True))
    centered = values - row_mean
    row_variance = lax.optimization_barrier(jnp.mean(centered * centered, axis=-1, keepdims=True))
    return (centered * lax.rsqrt(row_variance + epsilon) * gain).astype(jnp.bfloat16)

def one_head(head_inputs):
    queries, key_rows, value_rows = head_inputs
    scores = jnp.dot(queries, key_rows.T, preferred_element_type=jnp.float32) * HDIM ** (-0.5)
    unscaled = jnp.exp(scores - lax.optimization_barrier(jnp.max(scores, axis=1, keepdims=True)))
    totals = lax.optimization_barrier(jnp.sum(unscaled, axis=1, keepdims=True))
    weighted = jnp.dot(unscaled.astype(jnp.bfloat16), value_rows, preferred_element_type=jnp.float32)
    return (weighted / totals).astype(jnp.bfloat16)

def reference(patches, visible_count, visible_order, ln_gain, w_qkv, w_out):
    counts = visible_count.astype(jnp.int32)
    region_ends = jnp.cumsum(counts).astype(jnp.int32)
    region_starts = (region_ends - counts).astype(jnp.int32)
    block_ids = jnp.arange(TOTAL_BLK, dtype=jnp.int32)
    owners = lax.optimization_barrier(jnp.sum((region_ends[None, :] <= block_ids[:, None]).astype(jnp.int32), axis=1)).astype(jnp.int32)
    within_region = (block_ids - region_starts[owners]).astype(jnp.int32)
    source = (owners * BLK_DEV + visible_order[owners, within_region].astype(jnp.int32)).astype(jnp.int32)
    blocks = patches.reshape(N_CTX * BLK_DEV, BLOCK, D)
    packed = jnp.take(blocks, source, axis=0).reshape(TOTAL_ROWS, D)
    normed = layer_norm(packed, ln_gain)
    projected = jnp.dot(normed, w_qkv, preferred_element_type=jnp.float32).astype(jnp.bfloat16)
    split_heads = projected.reshape(TOTAL_ROWS, 3, HEADS, HDIM).transpose(1, 2, 0, 3)
    attended = lax.map(one_head, (split_heads[0], split_heads[1], split_heads[2]))
    attended = attended.transpose(1, 0, 2).reshape(TOTAL_ROWS, D)
    mixed_rows = (packed.astype(jnp.float32) + jnp.dot(attended, w_out, preferred_element_type=jnp.float32)).astype(jnp.bfloat16)
    return mixed_rows.reshape(TOTAL_BLK, N_CTX, BLOCK // N_CTX, D).transpose(1, 0, 2, 3).reshape(TOTAL_ROWS, D)
```

```python
import jax
import jax.numpy as jnp
from jax import lax
from jax.experimental import pallas as pl
from jax.experimental.pallas import tpu as pltpu
from jax.sharding import PartitionSpec as P

HEADS = 16
EPSILON = 1e-05
LOG2E = 1.4426950408889634
BF16 = jnp.bfloat16
F32 = jnp.float32


def select_kernel(order_ref, block_ref, out_ref):
    out_ref[...] = block_ref[...].reshape(out_ref.shape)


def select_blocks(order, patches, most, block_rows, devices):
    d_model = patches.shape[1]
    piece = block_rows // devices
    return pl.pallas_call(
        select_kernel,
        out_shape=jax.ShapeDtypeStruct((devices, most * piece, d_model), BF16),
        grid_spec=pltpu.PrefetchScalarGridSpec(
            num_scalar_prefetch=1,
            grid=(most,),
            in_specs=[pl.BlockSpec((block_rows, d_model), lambda j, order: (order[0, j], 0))],
            out_specs=pl.BlockSpec((devices, piece, d_model), lambda j, order: (0, j, 0)),
        ),
        name="select_blocks",
    )(order, patches)


def project_kernel(
    counts_ref, got_ref, gain_ref, wq_ref, wk_ref, wv_ref, packed_ref, out_ref, normed, slots
):
    total, most = slots.shape[0], got_ref.shape[0] // counts_ref.shape[0]
    piece = got_ref.shape[1]
    rows = normed.shape[0]
    half = rows // 2

    @pl.when(pl.program_id(0) == 0)
    def _():
        def find(k, state):
            region, within = state
            slots[k] = region * most + within
            last = within + 1 >= counts_ref[region]
            return (
                jnp.where(last, jnp.minimum(region + 1, counts_ref.shape[0] - 1), region),
                jnp.where(last, 0, within + 1),
            )

        lax.fori_loop(0, total, find, (jnp.int32(0), jnp.int32(0)))
        for k in range(total):
            packed_ref[k * piece : (k + 1) * piece, :] = got_ref[slots[k]]
        values = packed_ref[...].astype(F32)
        mean = jnp.mean(values, axis=-1, keepdims=True)
        centered = values - mean
        variance = jnp.mean(centered * centered, axis=-1, keepdims=True)
        normed[...] = (centered * lax.rsqrt(variance + EPSILON) * gain_ref[...]).astype(BF16)

    rows_in = normed[...]
    queries = jnp.dot(rows_in, wq_ref[...], preferred_element_type=F32)
    keys = jnp.dot(rows_in, wk_ref[...], preferred_element_type=F32)
    values = jnp.dot(rows_in, wv_ref[...], preferred_element_type=F32)
    keys_t = keys.T
    for h in range(out_ref.shape[0]):
        lanes = slice(h * 64, (h + 1) * 64)
        out_ref[h, :rows, :] = jnp.concatenate(
            [queries[:, lanes], values[:, lanes]], axis=1
        ).astype(BF16)
        out_ref[h, rows : rows + 64, :] = keys_t[lanes, :half].astype(BF16)
        out_ref[h, rows + 64 :, :] = keys_t[lanes, half:].astype(BF16)


def project(counts, got, gain, w_qkv, total):
    slot_count, piece, d_model = got.shape
    rows = total * piece
    groups = 4
    width = d_model // groups
    heads_group = HEADS // groups
    return pl.pallas_call(
        project_kernel,
        out_shape=(
            jax.ShapeDtypeStruct((rows, d_model), BF16),
            jax.ShapeDtypeStruct((HEADS, rows + 128, 128), BF16),
        ),
        grid_spec=pltpu.PrefetchScalarGridSpec(
            num_scalar_prefetch=1,
            grid=(groups,),
            in_specs=[
                pl.BlockSpec((slot_count, piece, d_model), lambda g, c: (0, 0, 0)),
                pl.BlockSpec((1, d_model), lambda g, c: (0, 0)),
                pl.BlockSpec((d_model, width), lambda g, c: (0, g)),
                pl.BlockSpec((d_model, width), lambda g, c: (0, groups + g)),
                pl.BlockSpec((d_model, width), lambda g, c: (0, 2 * groups + g)),
            ],
            out_specs=(
                pl.BlockSpec((rows, d_model), lambda g, c: (0, 0)),
                pl.BlockSpec((heads_group, rows + 128, 128), lambda g, c: (g, 0, 0)),
            ),
            scratch_shapes=[
                pltpu.VMEM((rows, d_model), BF16),
                pltpu.SMEM((total,), jnp.int32),
            ],
        ),
        name="project",
    )(counts, got, gain.reshape(1, d_model), w_qkv, w_qkv, w_qkv)


def attend_kernel(got_ref, out_ref, keys_t, values, scores):
    devices = got_ref.shape[0]
    rows = got_ref.shape[1] - 128
    half = rows // 2
    step = pl.program_id(0)

    @pl.when(step == 0)
    def _():
        keys_t[64:, :] = jnp.zeros((64, keys_t.shape[1]), BF16)
        lane = lax.broadcasted_iota(jnp.int32, (rows, 128), 1)
        for c in range(devices):
            values[c * rows : (c + 1) * rows, :] = jnp.where(
                lane < 64, jnp.ones((), BF16), got_ref[c, :rows, :]
            )
            keys_t[:64, c * rows : c * rows + half] = got_ref[c, rows : rows + 64, :]
            keys_t[:64, c * rows + half : (c + 1) * rows] = got_ref[c, rows + 64 :, :]

    queries = got_ref[step, :rows, :]
    width = 512
    chunks = keys_t.shape[1] // width
    top = None
    for j in range(chunks):
        part = jnp.dot(queries, keys_t[:, j * width : (j + 1) * width], preferred_element_type=F32)
        scores[:, j * width : (j + 1) * width] = part
        for b in range(width // 128):
            block = part[:, b * 128 : (b + 1) * 128]
            top = block if top is None else jnp.maximum(top, block)
    top = jnp.max(top, axis=1, keepdims=True)
    total = jnp.zeros((rows, 128), F32)
    for j in range(chunks):
        part = scores[:, j * width : (j + 1) * width]
        weights = jnp.exp2((part - top) * (0.125 * LOG2E)).astype(BF16)
        total = total + jnp.dot(
            weights, values[j * width : (j + 1) * width, :], preferred_element_type=F32
        )
    total_t = total.T
    out_ref[0] = (total_t[64:, :] / total_t[:64, :]).astype(BF16)


def attend(got):
    devices, packed_rows, lanes = got.shape
    rows = packed_rows - 128
    everything = devices * rows
    return pl.pallas_call(
        attend_kernel,
        out_shape=jax.ShapeDtypeStruct((devices, 64, rows), BF16),
        grid_spec=pltpu.PrefetchScalarGridSpec(
            num_scalar_prefetch=0,
            grid=(devices,),
            in_specs=[pl.BlockSpec((devices, packed_rows, lanes), lambda i: (0, 0, 0))],
            out_specs=pl.BlockSpec((1, 64, rows), lambda i: (i, 0, 0)),
            scratch_shapes=[
                pltpu.VMEM((128, everything), BF16),
                pltpu.VMEM((everything, 128), BF16),
                pltpu.VMEM((rows, everything), F32),
            ],
        ),
        name="attend",
    )(got)


def body(patches, visible_count, visible_order, ln_gain, w_qkv, w_out):
    devices = lax.axis_size("ctx")
    blocks_dev = visible_order.shape[1]
    block_rows = patches.shape[0] // blocks_dev
    d_model = patches.shape[1]
    total_blocks = devices * blocks_dev // 4
    most = min(3 * blocks_dev // 4, total_blocks - devices + 1)
    piece = block_rows // devices

    chosen = select_blocks(visible_order, patches, most, block_rows, devices)
    received = lax.all_to_all(chosen, "ctx", split_axis=0, concat_axis=0, tiled=True)
    received = received.reshape(devices * most, piece, d_model)
    packed, projected = project(visible_count, received, ln_gain, w_qkv, total_blocks)
    by_head = lax.all_to_all(projected, "ctx", split_axis=0, concat_axis=0, tiled=True)
    attended = attend(by_head)
    attended = lax.all_to_all(attended, "ctx", split_axis=0, concat_axis=0, tiled=True)
    attended = attended.reshape(d_model, total_blocks * piece)
    mixed = packed.astype(F32) + lax.dot_general(
        attended, w_out, (((0,), (0,)), ((), ())), preferred_element_type=F32
    )
    return mixed.astype(BF16)


def solution(mesh):
    return jax.shard_map(
        body,
        mesh=mesh,
        in_specs=(P(("dp", "ctx"), None), P("dp"), P(("dp", "ctx"), None), P(), P(), P()),
        out_specs=P(("dp", "ctx"), None),
        check_vma=False,
    )
```

```python
import jax
import jax.numpy as jnp
from jax import lax
from jax.experimental import pallas as pl
from jax.experimental.pallas import tpu as pltpu
from jax.sharding import PartitionSpec as P

HEADS = 16
EPSILON = 1e-05
LOG2E = 1.4426950408889634
BF16 = jnp.bfloat16
F32 = jnp.float32


def select_kernel(order_ref, patches_ref, out_ref, sems):
    devices, rows, _ = out_ref.shape
    most = sems.shape[0]
    piece = rows // most
    copies = []
    for j in range(most):
        source = patches_ref.at[pl.ds(order_ref[0, j] * devices, devices)]
        target = out_ref.at[:, j * piece : (j + 1) * piece, :]
        copies.append(pltpu.make_async_copy(source, target, sems.at[j]))
    for copy in copies:
        copy.start()
    for copy in copies:
        copy.wait()


def select_blocks(order, patches, most, block_rows, devices):
    d_model = patches.shape[1]
    piece = block_rows // devices
    return pl.pallas_call(
        select_kernel,
        out_shape=jax.ShapeDtypeStruct((devices, most * piece, d_model), BF16),
        in_specs=[
            pl.BlockSpec(memory_space=pltpu.SMEM),
            pl.BlockSpec(memory_space=pltpu.HBM),
        ],
        out_specs=pl.BlockSpec(memory_space=pltpu.VMEM),
        scratch_shapes=[pltpu.SemaphoreType.DMA((most,))],
        compiler_params=pltpu.CompilerParams(vmem_limit_bytes=8 << 20),
        name="select_blocks",
    )(order, patches.reshape(patches.shape[0] // piece, piece, d_model))


def project_kernel(
    counts_ref, got_ref, gain_ref, wq_ref, wk_ref, wv_ref, packed_ref, out_ref, normed, slots
):
    total, most = slots.shape[0], got_ref.shape[0] // counts_ref.shape[0]
    piece = got_ref.shape[1]
    rows = normed.shape[0]
    half = rows // 2

    @pl.when(pl.program_id(0) == 0)
    def _():
        def find(k, state):
            region, within = state
            slots[k] = region * most + within
            last = within + 1 >= counts_ref[region]
            return (
                jnp.where(last, jnp.minimum(region + 1, counts_ref.shape[0] - 1), region),
                jnp.where(last, 0, within + 1),
            )

        lax.fori_loop(0, total, find, (jnp.int32(0), jnp.int32(0)))
        for k in range(total):
            packed_ref[k * piece : (k + 1) * piece, :] = got_ref[slots[k]]
        values = packed_ref[...].astype(F32)
        mean = jnp.mean(values, axis=-1, keepdims=True)
        centered = values - mean
        variance = jnp.mean(centered * centered, axis=-1, keepdims=True)
        normed[...] = (centered * lax.rsqrt(variance + EPSILON) * gain_ref[...]).astype(BF16)

    rows_in = normed[...]
    queries = jnp.dot(rows_in, wq_ref[...], preferred_element_type=F32)
    keys = jnp.dot(rows_in, wk_ref[...], preferred_element_type=F32)
    values = jnp.dot(rows_in, wv_ref[...], preferred_element_type=F32)
    queries_t = queries.T
    values_t = values.T
    for h in range(out_ref.shape[0]):
        lanes = slice(h * 64, (h + 1) * 64)
        out_ref[h, :half, :] = jnp.concatenate(
            [keys[:half, lanes], keys[half:, lanes]], axis=1
        ).astype(BF16)
        out_ref[h, half : half + 64, :] = queries_t[lanes, :half].astype(BF16)
        out_ref[h, half + 64 : rows, :] = queries_t[lanes, half:].astype(BF16)
        out_ref[h, rows : rows + 64, :] = values_t[lanes, :half].astype(BF16)
        out_ref[h, rows + 64 :, :] = values_t[lanes, half:].astype(BF16)


def project(counts, got, gain, w_qkv, total):
    slot_count, piece, d_model = got.shape
    rows = total * piece
    groups = 4
    width = d_model // groups
    heads_group = HEADS // groups
    return pl.pallas_call(
        project_kernel,
        out_shape=(
            jax.ShapeDtypeStruct((rows, d_model), BF16),
            jax.ShapeDtypeStruct((HEADS, rows + 128, 128), BF16),
        ),
        grid_spec=pltpu.PrefetchScalarGridSpec(
            num_scalar_prefetch=1,
            grid=(groups,),
            in_specs=[
                pl.BlockSpec((slot_count, piece, d_model), lambda g, c: (0, 0, 0)),
                pl.BlockSpec((1, d_model), lambda g, c: (0, 0)),
                pl.BlockSpec((d_model, width), lambda g, c: (0, g)),
                pl.BlockSpec((d_model, width), lambda g, c: (0, groups + g)),
                pl.BlockSpec((d_model, width), lambda g, c: (0, 2 * groups + g)),
            ],
            out_specs=(
                pl.BlockSpec((rows, d_model), lambda g, c: (0, 0)),
                pl.BlockSpec((heads_group, rows + 128, 128), lambda g, c: (g, 0, 0)),
            ),
            scratch_shapes=[
                pltpu.VMEM((rows, d_model), BF16),
                pltpu.SMEM((total,), jnp.int32),
            ],
        ),
        compiler_params=pltpu.CompilerParams(vmem_limit_bytes=24 << 20),
        name="project",
    )(counts, got, gain.reshape(1, d_model), w_qkv, w_qkv, w_qkv)


def attend_kernel(got_ref, out_ref, values_t, scores_a, scores_b, top_ref):
    step = pl.program_id(0)
    devices = got_ref.shape[0]
    rows = out_ref.shape[2]
    half = rows // 2
    zero = jnp.zeros((64, rows), BF16)

    def key_weights(i):
        queries_t = jnp.concatenate([got_ref[i, 128:192, :], got_ref[i, 192:256, :]], axis=1)
        return (
            jnp.concatenate([queries_t, zero], axis=0),
            jnp.concatenate([zero, queries_t], axis=0),
        )

    def score(weights, scores, c, top):
        key_rows = got_ref[c, :128, :]
        for h in range(2):
            part = jnp.dot(key_rows, weights[h], preferred_element_type=F32)
            scores[c * rows + h * half : c * rows + (h + 1) * half, :] = part
            for b in range(half // 8):
                block = part[b * 8 : (b + 1) * 8]
                top = block if top is None else jnp.maximum(top, block)
        return top

    def weigh(scores, c, top, total):
        part = scores[c * rows : (c + 1) * rows, :]
        probs = jnp.exp2((part - top) * (0.125 * LOG2E)).astype(BF16)
        weighted = jnp.dot(
            values_t[:, c * rows : (c + 1) * rows], probs, preferred_element_type=F32
        )
        return weighted if total is None else total + weighted

    def keep(top):
        top_ref[...] = jnp.broadcast_to(jnp.max(top, axis=0, keepdims=True), top_ref.shape)

    @pl.when(step == 0)
    def _():
        for c in range(devices):
            values_t[:64, c * rows : c * rows + half] = got_ref[c, 256:320, :]
            values_t[:64, c * rows + half : (c + 1) * rows] = got_ref[c, 320:384, :]
        values_t[64:, :] = jnp.ones((values_t.shape[0] - 64, values_t.shape[1]), BF16)
        top = None
        weights = key_weights(0)
        for c in range(devices):
            top = score(weights, scores_a, c, top)
        keep(top)

    def phase(current, following):
        top = top_ref[:1, :]
        total = next_top = None
        if following is not None:
            weights = key_weights(jnp.minimum(step + 1, devices - 1))
        for c in range(devices):
            if following is not None:
                next_top = score(weights, following, c, next_top)
            total = weigh(current, c, top, total)
        if following is not None:
            keep(next_top)
        out_ref[0] = (total[:64] / total[64:65]).astype(BF16)

    even = step % 2 == 0
    live = step < devices - 1
    pl.when(even & live)(lambda: phase(scores_a, scores_b))
    pl.when(jnp.logical_not(even) & live)(lambda: phase(scores_b, scores_a))
    pl.when(jnp.logical_not(live))(
        lambda: phase(scores_a if devices % 2 else scores_b, None)
    )


def attend(got):
    devices, packed_rows, lanes = got.shape
    rows = 256
    everything = devices * rows
    return pl.pallas_call(
        attend_kernel,
        out_shape=jax.ShapeDtypeStruct((devices, 64, rows), BF16),
        grid_spec=pltpu.PrefetchScalarGridSpec(
            num_scalar_prefetch=0,
            grid=(devices,),
            in_specs=[pl.BlockSpec((devices, packed_rows, lanes), lambda i: (0, 0, 0))],
            out_specs=pl.BlockSpec((1, 64, rows), lambda i: (i, 0, 0)),
            scratch_shapes=[
                pltpu.VMEM((80, everything), BF16),
                pltpu.VMEM((everything, rows), F32),
                pltpu.VMEM((everything, rows), F32),
                pltpu.VMEM((8, rows), F32),
            ],
        ),
        compiler_params=pltpu.CompilerParams(vmem_limit_bytes=24 << 20),
        name="attend",
    )(got)


def body(patches, visible_count, visible_order, ln_gain, w_qkv, w_out):
    devices = lax.axis_size("ctx")
    blocks_dev = visible_order.shape[1]
    block_rows = patches.shape[0] // blocks_dev
    d_model = patches.shape[1]
    total_blocks = devices * blocks_dev // 4
    most = min(3 * blocks_dev // 4, total_blocks - devices + 1)
    piece = block_rows // devices

    chosen = select_blocks(visible_order, patches, most, block_rows, devices)
    received = lax.all_to_all(chosen, "ctx", split_axis=0, concat_axis=0, tiled=True)
    received = received.reshape(devices * most, piece, d_model)
    packed, projected = project(visible_count, received, ln_gain, w_qkv, total_blocks)
    by_head = lax.all_to_all(projected, "ctx", split_axis=0, concat_axis=0, tiled=True)
    attended = attend(by_head)
    attended = lax.all_to_all(attended, "ctx", split_axis=0, concat_axis=0, tiled=True)
    attended = attended.reshape(d_model, total_blocks * piece)
    mixed = packed.astype(F32) + lax.dot_general(
        attended, w_out, (((0,), (0,)), ((), ())), preferred_element_type=F32
    )
    return mixed.astype(BF16)


def solution(mesh):
    return jax.shard_map(
        body,
        mesh=mesh,
        in_specs=(P(("dp", "ctx"), None), P("dp"), P(("dp", "ctx"), None), P(), P(), P()),
        out_specs=P(("dp", "ctx"), None),
        check_vma=False,
    )
```

```python
import jax
import jax.numpy as jnp
from jax import lax
from jax.experimental import pallas as pl
from jax.experimental.pallas import tpu as pltpu
from jax.sharding import PartitionSpec as P

HEADS = 16
EPSILON = 1e-05
LOG2E = 1.4426950408889634
BF16 = jnp.bfloat16
F32 = jnp.float32


def select_kernel(order_ref, patches_ref, out_ref, sems):
    devices, rows, _ = out_ref.shape
    most = sems.shape[0]
    piece = rows // most
    copies = []
    for j in range(most):
        source = patches_ref.at[pl.ds(order_ref[0, j] * devices, devices)]
        target = out_ref.at[:, j * piece : (j + 1) * piece, :]
        copies.append(pltpu.make_async_copy(source, target, sems.at[j]))
    for copy in copies:
        copy.start()
    for copy in copies:
        copy.wait()


def select_blocks(order, patches, most, block_rows, devices):
    d_model = patches.shape[1]
    piece = block_rows // devices
    return pl.pallas_call(
        select_kernel,
        out_shape=jax.ShapeDtypeStruct((devices, most * piece, d_model), BF16),
        in_specs=[
            pl.BlockSpec(memory_space=pltpu.SMEM),
            pl.BlockSpec(memory_space=pltpu.HBM),
        ],
        out_specs=pl.BlockSpec(memory_space=pltpu.VMEM),
        scratch_shapes=[pltpu.SemaphoreType.DMA((most,))],
        compiler_params=pltpu.CompilerParams(vmem_limit_bytes=8 << 20),
        name="select_blocks",
    )(
        order,
        pltpu.with_memory_space_constraint(
            patches.reshape(patches.shape[0] // piece, piece, d_model), pltpu.HBM
        ),
    )


def project_kernel(
    counts_ref, got_ref, gain_ref, weights_ref, packed_ref, out_ref, normed, slots
):
    total, most = slots.shape[0], got_ref.shape[0] // counts_ref.shape[0]
    piece = got_ref.shape[1]
    rows, d_model = normed.shape
    half = rows // 2

    def find(k, state):
        region, within = state
        slots[k] = region * most + within
        last = within + 1 >= counts_ref[region]
        return (
            jnp.where(last, jnp.minimum(region + 1, counts_ref.shape[0] - 1), region),
            jnp.where(last, 0, within + 1),
        )

    lax.fori_loop(0, total, find, (jnp.int32(0), jnp.int32(0)))
    for k in range(total):
        packed_ref[k * piece : (k + 1) * piece, :] = got_ref[slots[k]]
    values = packed_ref[...].astype(F32)
    mean = jnp.mean(values, axis=-1, keepdims=True)
    centered = values - mean
    variance = jnp.mean(centered * centered, axis=-1, keepdims=True)
    normed[...] = (centered * lax.rsqrt(variance + EPSILON) * gain_ref[...]).astype(BF16)

    width = 256
    rows_in = normed[...]

    def columns(group, start):
        lanes = pl.ds(pl.multiple_of(start + group * width, width), width)
        return jnp.dot(rows_in, weights_ref[:, lanes], preferred_element_type=F32)

    def group_step(group, _):
        queries_t = columns(group, 0).T
        keys = columns(group, d_model)
        values_t = columns(group, 2 * d_model).T
        for h in range(width // 64):
            lanes = slice(h * 64, (h + 1) * 64)
            head = group * (width // 64) + h
            out_ref[head, :half, :] = jnp.concatenate(
                [keys[:half, lanes], keys[half:, lanes]], axis=1
            ).astype(BF16)
            out_ref[head, half : half + 64, :] = queries_t[lanes, :half].astype(BF16)
            out_ref[head, half + 64 : rows, :] = queries_t[lanes, half:].astype(BF16)
            out_ref[head, rows : rows + 64, :] = values_t[lanes, :half].astype(BF16)
            out_ref[head, rows + 64 :, :] = values_t[lanes, half:].astype(BF16)
        return 0

    for group in range(d_model // width):
        group_step(group, 0)


def project(counts, got, gain, w_qkv, total):
    slot_count, piece, d_model = got.shape
    rows = total * piece
    in_vmem = pl.BlockSpec(memory_space=pltpu.VMEM)
    return pl.pallas_call(
        project_kernel,
        out_shape=(
            jax.ShapeDtypeStruct((rows, d_model), BF16),
            jax.ShapeDtypeStruct((HEADS, rows + 128, 128), BF16),
        ),
        in_specs=[pl.BlockSpec(memory_space=pltpu.SMEM), in_vmem, in_vmem, in_vmem],
        out_specs=(in_vmem, in_vmem),
        scratch_shapes=[
            pltpu.VMEM((rows, d_model), BF16),
            pltpu.SMEM((total,), jnp.int32),
        ],
        compiler_params=pltpu.CompilerParams(vmem_limit_bytes=24 << 20),
        name="project",
    )(counts, got, gain.reshape(1, d_model), w_qkv)


def attend_kernel(got_ref, out_ref, values_t, scores_a, scores_b, top_ref):
    devices = got_ref.shape[0]
    rows = out_ref.shape[2]
    half = rows // 2
    zero = jnp.zeros((64, rows), BF16)

    def key_weights(i):
        queries_t = jnp.concatenate([got_ref[i, 128:192, :], got_ref[i, 192:256, :]], axis=1)
        return (
            jnp.concatenate([queries_t, zero], axis=0),
            jnp.concatenate([zero, queries_t], axis=0),
        )

    def score(weights, scores, c, top):
        key_rows = got_ref[c, :128, :]
        for h in range(2):
            part = jnp.dot(key_rows, weights[h], preferred_element_type=F32)
            scores[c * rows + h * half : c * rows + (h + 1) * half, :] = part
            for b in range(half // 8):
                block = part[b * 8 : (b + 1) * 8]
                top = block if top is None else jnp.maximum(top, block)
        return top

    def weigh(scores, c, top, total):
        part = scores[c * rows : (c + 1) * rows, :]
        probs = jnp.exp2((part - top) * (0.125 * LOG2E)).astype(BF16)
        weighted = jnp.dot(
            values_t[:, c * rows : (c + 1) * rows], probs, preferred_element_type=F32
        )
        return weighted if total is None else total + weighted

    def keep(top):
        top_ref[...] = jnp.broadcast_to(jnp.max(top, axis=0, keepdims=True), top_ref.shape)

    for c in range(devices):
        values_t[:64, c * rows : c * rows + half] = got_ref[c, 256:320, :]
        values_t[:64, c * rows + half : (c + 1) * rows] = got_ref[c, 320:384, :]
    values_t[64:, :] = jnp.ones((values_t.shape[0] - 64, values_t.shape[1]), BF16)
    first_top = None
    first_weights = key_weights(0)
    for c in range(devices):
        first_top = score(first_weights, scores_a, c, first_top)
    keep(first_top)

    def phase(step, current, following):
        top = top_ref[:1, :]
        total = next_top = None
        if following is not None:
            weights = key_weights(step + 1)
        for c in range(devices):
            if following is not None:
                next_top = score(weights, following, c, next_top)
            total = weigh(current, c, top, total)
        if following is not None:
            keep(next_top)
        out_ref[step] = (total[:64] / total[64:65]).astype(BF16)

    @pl.loop(0, devices - 1)
    def _(step):
        even = step % 2 == 0
        pl.when(even)(lambda: phase(step, scores_a, scores_b))
        pl.when(jnp.logical_not(even))(lambda: phase(step, scores_b, scores_a))

    phase(devices - 1, scores_a if devices % 2 else scores_b, None)


def attend(got):
    devices, packed_rows, lanes = got.shape
    rows = 256
    everything = devices * rows
    return pl.pallas_call(
        attend_kernel,
        out_shape=jax.ShapeDtypeStruct((devices, 64, rows), BF16),
        in_specs=[pl.BlockSpec(memory_space=pltpu.VMEM)],
        out_specs=pl.BlockSpec(memory_space=pltpu.VMEM),
        scratch_shapes=[
            pltpu.VMEM((80, everything), BF16),
            pltpu.VMEM((everything, rows), F32),
            pltpu.VMEM((everything, rows), F32),
            pltpu.VMEM((8, rows), F32),
        ],
        compiler_params=pltpu.CompilerParams(vmem_limit_bytes=24 << 20),
        name="attend",
    )(got)


def body(patches, visible_count, visible_order, ln_gain, w_qkv, w_out):
    devices = lax.axis_size("ctx")
    blocks_dev = visible_order.shape[1]
    block_rows = patches.shape[0] // blocks_dev
    d_model = patches.shape[1]
    total_blocks = devices * blocks_dev // 4
    most = min(3 * blocks_dev // 4, total_blocks - devices + 1)
    piece = block_rows // devices

    chosen = select_blocks(visible_order, patches, most, block_rows, devices)
    received = lax.all_to_all(chosen, "ctx", split_axis=0, concat_axis=0, tiled=True)
    received = received.reshape(devices * most, piece, d_model)
    packed, projected = project(visible_count, received, ln_gain, w_qkv, total_blocks)
    by_head = lax.all_to_all(projected, "ctx", split_axis=0, concat_axis=0, tiled=True)
    attended = attend(by_head)
    attended = lax.all_to_all(attended, "ctx", split_axis=0, concat_axis=0, tiled=True)
    attended = attended.reshape(d_model, total_blocks * piece)
    mixed = packed.astype(F32) + lax.dot_general(
        attended, w_out, (((0,), (0,)), ((), ())), preferred_element_type=F32
    )
    return mixed.astype(BF16)


def solution(mesh):
    return jax.shard_map(
        body,
        mesh=mesh,
        in_specs=(P(("dp", "ctx"), None), P("dp"), P(("dp", "ctx"), None), P(), P(), P()),
        out_specs=P(("dp", "ctx"), None),
        check_vma=False,
    )
```

```python
import jax
import jax.numpy as jnp
from jax import lax
from jax.experimental import pallas as pl
from jax.experimental.pallas import tpu as pltpu
from jax.sharding import PartitionSpec as P

HEADS = 16
EPSILON = 1e-05
LOG2E = 1.4426950408889634
STAGGER_NS = 20000
BF16 = jnp.bfloat16
F32 = jnp.float32


def select_kernel(order_ref, patches_ref, out_ref, sems):
    devices, rows, _ = out_ref.shape
    most = sems.shape[0]
    piece = rows // most
    copies = []
    for j in range(most):
        source = patches_ref.at[pl.ds(order_ref[0, j] * devices, devices)]
        target = out_ref.at[:, j * piece : (j + 1) * piece, :]
        copies.append(pltpu.make_async_copy(source, target, sems.at[j]))
    for copy in copies:
        copy.start()
    pl.when(lax.axis_index("dp") % 2 == 1)(lambda: pl.delay(STAGGER_NS))
    for copy in copies:
        copy.wait()


def select_blocks(order, patches, most, block_rows, devices):
    d_model = patches.shape[1]
    piece = block_rows // devices
    return pl.pallas_call(
        select_kernel,
        out_shape=jax.ShapeDtypeStruct((devices, most * piece, d_model), BF16),
        in_specs=[
            pl.BlockSpec(memory_space=pltpu.SMEM),
            pl.BlockSpec(memory_space=pltpu.HBM),
        ],
        out_specs=pl.BlockSpec(memory_space=pltpu.VMEM),
        scratch_shapes=[pltpu.SemaphoreType.DMA((most,))],
        compiler_params=pltpu.CompilerParams(vmem_limit_bytes=8 << 20),
        name="select_blocks",
    )(
        order,
        pltpu.with_memory_space_constraint(
            patches.reshape(patches.shape[0] // piece, piece, d_model), pltpu.HBM
        ),
    )


def project_kernel(
    counts_ref, got_ref, gain_ref, weights_ref, packed_ref, out_ref, normed, slots
):
    total, most = slots.shape[0], got_ref.shape[0] // counts_ref.shape[0]
    piece = got_ref.shape[1]
    rows, d_model = normed.shape
    half = rows // 2

    def find(k, state):
        region, within = state
        slots[k] = region * most + within
        last = within + 1 >= counts_ref[region]
        return (
            jnp.where(last, jnp.minimum(region + 1, counts_ref.shape[0] - 1), region),
            jnp.where(last, 0, within + 1),
        )

    lax.fori_loop(0, total, find, (jnp.int32(0), jnp.int32(0)))
    for k in range(total):
        packed_ref[k * piece : (k + 1) * piece, :] = got_ref[slots[k]]
    values = packed_ref[...].astype(F32)
    mean = jnp.mean(values, axis=-1, keepdims=True)
    centered = values - mean
    variance = jnp.mean(centered * centered, axis=-1, keepdims=True)
    normed[...] = (centered * lax.rsqrt(variance + EPSILON) * gain_ref[...]).astype(BF16)

    width = 256
    rows_in = normed[...]

    def columns(group, start):
        lanes = pl.ds(pl.multiple_of(start + group * width, width), width)
        return jnp.dot(rows_in, weights_ref[:, lanes], preferred_element_type=F32)

    def group_step(group, _):
        queries_t = columns(group, 0).T
        keys = columns(group, d_model)
        values_t = columns(group, 2 * d_model).T
        for h in range(width // 64):
            lanes = slice(h * 64, (h + 1) * 64)
            head = group * (width // 64) + h
            out_ref[head, :half, :] = jnp.concatenate(
                [keys[:half, lanes], keys[half:, lanes]], axis=1
            ).astype(BF16)
            out_ref[head, half : half + 64, :] = queries_t[lanes, :half].astype(BF16)
            out_ref[head, half + 64 : rows, :] = queries_t[lanes, half:].astype(BF16)
            out_ref[head, rows : rows + 64, :] = values_t[lanes, :half].astype(BF16)
            out_ref[head, rows + 64 :, :] = values_t[lanes, half:].astype(BF16)
        return 0

    for group in range(d_model // width):
        group_step(group, 0)


def project(counts, got, gain, w_qkv, total):
    slot_count, piece, d_model = got.shape
    rows = total * piece
    in_vmem = pl.BlockSpec(memory_space=pltpu.VMEM)
    return pl.pallas_call(
        project_kernel,
        out_shape=(
            jax.ShapeDtypeStruct((rows, d_model), BF16),
            jax.ShapeDtypeStruct((HEADS, rows + 128, 128), BF16),
        ),
        in_specs=[pl.BlockSpec(memory_space=pltpu.SMEM), in_vmem, in_vmem, in_vmem],
        out_specs=(in_vmem, in_vmem),
        scratch_shapes=[
            pltpu.VMEM((rows, d_model), BF16),
            pltpu.SMEM((total,), jnp.int32),
        ],
        compiler_params=pltpu.CompilerParams(vmem_limit_bytes=24 << 20),
        name="project",
    )(counts, got, gain.reshape(1, d_model), w_qkv)


def attend_kernel(got_ref, out_ref, values_t, scores_a, scores_b, top_ref):
    devices = got_ref.shape[0]
    rows = out_ref.shape[2]
    half = rows // 2
    zero = jnp.zeros((64, rows), BF16)

    def key_weights(i):
        queries_t = jnp.concatenate([got_ref[i, 128:192, :], got_ref[i, 192:256, :]], axis=1)
        return (
            jnp.concatenate([queries_t, zero], axis=0),
            jnp.concatenate([zero, queries_t], axis=0),
        )

    def score(weights, scores, c, top):
        key_rows = got_ref[c, :128, :]
        for h in range(2):
            part = jnp.dot(key_rows, weights[h], preferred_element_type=F32)
            scores[c * rows + h * half : c * rows + (h + 1) * half, :] = part
            for b in range(half // 8):
                block = part[b * 8 : (b + 1) * 8]
                top = block if top is None else jnp.maximum(top, block)
        return top

    def weigh(scores, c, top, total):
        part = scores[c * rows : (c + 1) * rows, :]
        probs = jnp.exp2((part - top) * (0.125 * LOG2E)).astype(BF16)
        weighted = jnp.dot(
            values_t[:, c * rows : (c + 1) * rows], probs, preferred_element_type=F32
        )
        return weighted if total is None else total + weighted

    def keep(top):
        top_ref[...] = jnp.broadcast_to(jnp.max(top, axis=0, keepdims=True), top_ref.shape)

    for c in range(devices):
        values_t[:64, c * rows : c * rows + half] = got_ref[c, 256:320, :]
        values_t[:64, c * rows + half : (c + 1) * rows] = got_ref[c, 320:384, :]
    values_t[64:, :] = jnp.ones((values_t.shape[0] - 64, values_t.shape[1]), BF16)
    first_top = None
    first_weights = key_weights(0)
    for c in range(devices):
        first_top = score(first_weights, scores_a, c, first_top)
    keep(first_top)

    def phase(step, current, following):
        top = top_ref[:1, :]
        total = next_top = None
        if following is not None:
            weights = key_weights(step + 1)
        for c in range(devices):
            if following is not None:
                next_top = score(weights, following, c, next_top)
            total = weigh(current, c, top, total)
        if following is not None:
            keep(next_top)
        out_ref[step] = (total[:64] / total[64:65]).astype(BF16)

    @pl.loop(0, devices - 1)
    def _(step):
        even = step % 2 == 0
        pl.when(even)(lambda: phase(step, scores_a, scores_b))
        pl.when(jnp.logical_not(even))(lambda: phase(step, scores_b, scores_a))

    phase(devices - 1, scores_a if devices % 2 else scores_b, None)


def attend(got):
    devices, packed_rows, lanes = got.shape
    rows = 256
    everything = devices * rows
    return pl.pallas_call(
        attend_kernel,
        out_shape=jax.ShapeDtypeStruct((devices, 64, rows), BF16),
        in_specs=[pl.BlockSpec(memory_space=pltpu.VMEM)],
        out_specs=pl.BlockSpec(memory_space=pltpu.VMEM),
        scratch_shapes=[
            pltpu.VMEM((80, everything), BF16),
            pltpu.VMEM((everything, rows), F32),
            pltpu.VMEM((everything, rows), F32),
            pltpu.VMEM((8, rows), F32),
        ],
        compiler_params=pltpu.CompilerParams(vmem_limit_bytes=24 << 20),
        name="attend",
    )(got)


def body(patches, visible_count, visible_order, ln_gain, w_qkv, w_out):
    devices = lax.axis_size("ctx")
    blocks_dev = visible_order.shape[1]
    block_rows = patches.shape[0] // blocks_dev
    d_model = patches.shape[1]
    total_blocks = devices * blocks_dev // 4
    most = min(3 * blocks_dev // 4, total_blocks - devices + 1)
    piece = block_rows // devices

    chosen = select_blocks(visible_order, patches, most, block_rows, devices)
    received = lax.all_to_all(chosen, "ctx", split_axis=0, concat_axis=0, tiled=True)
    received = received.reshape(devices * most, piece, d_model)
    packed, projected = project(visible_count, received, ln_gain, w_qkv, total_blocks)
    by_head = lax.all_to_all(projected, "ctx", split_axis=0, concat_axis=0, tiled=True)
    attended = attend(by_head)
    attended = lax.all_to_all(attended, "ctx", split_axis=0, concat_axis=0, tiled=True)
    attended = attended.reshape(d_model, total_blocks * piece)
    mixed = packed.astype(F32) + lax.dot_general(
        attended, w_out, (((0,), (0,)), ((), ())), preferred_element_type=F32
    )
    return mixed.astype(BF16)


def solution(mesh):
    return jax.shard_map(
        body,
        mesh=mesh,
        in_specs=(P(("dp", "ctx"), None), P("dp"), P(("dp", "ctx"), None), P(), P(), P()),
        out_specs=P(("dp", "ctx"), None),
        check_vma=False,
    )
```

```python
import jax
import jax.numpy as jnp
from jax import lax
from jax.experimental import pallas as pl
from jax.experimental.pallas import tpu as pltpu
from jax.sharding import PartitionSpec as P

HEADS = 16
EPSILON = 1e-05
LOG2E = 1.4426950408889634
STAGGER_NS = 20000
BF16 = jnp.bfloat16
F32 = jnp.float32


def select_kernel(order_ref, patches_ref, rest_ref, home_ref, sems):
    devices, rows, _ = rest_ref.shape
    most = sems.shape[0]
    piece = rows // (most - 1)
    copies = []
    for j in range(most):
        source = patches_ref.at[pl.ds(order_ref[0, j] * devices, devices)]
        target = rest_ref.at[:, (j - 1) * piece : j * piece, :] if j else home_ref
        copies.append(pltpu.make_async_copy(source, target, sems.at[j]))
    for copy in copies:
        copy.start()
    pl.when(lax.axis_index("dp") % 2 == 1)(lambda: pl.delay(STAGGER_NS))
    for copy in copies:
        copy.wait()


def select_blocks(order, patches, most, block_rows, devices):
    d_model = patches.shape[1]
    piece = block_rows // devices
    in_vmem = pl.BlockSpec(memory_space=pltpu.VMEM)
    return pl.pallas_call(
        select_kernel,
        out_shape=(
            jax.ShapeDtypeStruct((devices, (most - 1) * piece, d_model), BF16),
            jax.ShapeDtypeStruct((devices, piece, d_model), BF16),
        ),
        in_specs=[
            pl.BlockSpec(memory_space=pltpu.SMEM),
            pl.BlockSpec(memory_space=pltpu.HBM),
        ],
        out_specs=(in_vmem, in_vmem),
        scratch_shapes=[pltpu.SemaphoreType.DMA((most,))],
        compiler_params=pltpu.CompilerParams(vmem_limit_bytes=8 << 20),
        name="select_blocks",
    )(
        order,
        pltpu.with_memory_space_constraint(
            patches.reshape(patches.shape[0] // piece, piece, d_model), pltpu.HBM
        ),
    )


def walk_blocks(counts_ref, total, visit):
    def step(k, state):
        region, within, others = state
        visit(k, region, within, others)
        last = within + 1 >= counts_ref[region]
        return (
            jnp.where(last, jnp.minimum(region + 1, counts_ref.shape[0] - 1), region),
            jnp.where(last, 0, within + 1),
            jnp.where(within > 0, others + 1, others),
        )

    lax.fori_loop(0, total, step, (jnp.int32(0), jnp.int32(0), jnp.int32(0)))


def normalize(rows_in, gain):
    values = rows_in.astype(F32)
    mean = jnp.mean(values, axis=-1, keepdims=True)
    centered = values - mean
    variance = jnp.mean(centered * centered, axis=-1, keepdims=True)
    return (centered * lax.rsqrt(variance + EPSILON) * gain).astype(BF16)


def project_kernel(
    counts_ref,
    got_ref,
    home_ref,
    gain_ref,
    weights_ref,
    packed_ref,
    out_ref,
    normed,
    held,
    slots,
    sems,
):
    regions, piece, d_model = home_ref.shape
    per_region = got_ref.shape[0] // regions
    half = packed_ref.shape[0]
    blocks = half // piece
    width = held.shape[2]
    starts = [t * d_model + g for g in range(0, d_model, width) for t in range(3)]
    copies = [
        pltpu.make_async_copy(weights_ref.at[:, start : start + width], held.at[i], sems.at[i])
        for i, start in enumerate(starts)
    ]
    for copy in copies:
        copy.start()

    def visit(block, region, within, others):
        slots[others] = region * per_region + jnp.maximum(within, 1) - 1

    walk_blocks(counts_ref, blocks + regions, visit)
    for k in range(blocks):
        packed_ref[k * piece : (k + 1) * piece, :] = got_ref[slots[k]]
    normed[:half, :] = normalize(home_ref[...].reshape(half, d_model), gain_ref[...])
    normed[half:, :] = normalize(packed_ref[...], gain_ref[...])

    rows_in = normed[...]

    def columns(i):
        copies[i].wait()
        return jnp.dot(rows_in, held[i], preferred_element_type=F32)

    for start in range(0, d_model, width):
        i = start // width * 3
        queries_t = columns(i).T
        keys = columns(i + 1)
        values_t = columns(i + 2).T
        for h in range(width // 64):
            head = start // 64 + h
            lanes = slice(h * 64, (h + 1) * 64)
            out_ref[head, :half, :] = jnp.concatenate(
                [keys[:half, lanes], keys[half:, lanes]], axis=1
            ).astype(BF16)
            for part, values in ((half, queries_t), (half + 128, values_t)):
                out_ref[head, part : part + 64, :] = values[lanes, :half].astype(BF16)
                out_ref[head, part + 64 : part + 128, :] = values[lanes, half:].astype(BF16)


def project(counts, got, home, gain, w_qkv, blocks):
    _, piece, d_model = got.shape
    half = blocks * piece
    in_vmem = pl.BlockSpec(memory_space=pltpu.VMEM)
    return pl.pallas_call(
        project_kernel,
        out_shape=(
            jax.ShapeDtypeStruct((half, d_model), BF16),
            jax.ShapeDtypeStruct((HEADS, half + 256, 128), BF16),
        ),
        in_specs=[pl.BlockSpec(memory_space=pltpu.SMEM)]
        + [in_vmem] * 3
        + [pl.BlockSpec(memory_space=pltpu.HBM)],
        out_specs=(in_vmem, in_vmem),
        scratch_shapes=[
            pltpu.VMEM((2 * half, d_model), BF16),
            pltpu.VMEM((3 * d_model // 256, d_model, 256), BF16),
            pltpu.SMEM((blocks + 1,), jnp.int32),
            pltpu.SemaphoreType.DMA((3 * d_model // 256,)),
        ],
        compiler_params=pltpu.CompilerParams(vmem_limit_bytes=24 << 20),
        name="project",
    )(counts, got, home, gain, pltpu.with_memory_space_constraint(w_qkv, pltpu.HBM))


def attend_kernel(got_ref, home_ref, out_ref, values_t, scores_a, scores_b, top_ref, even_ref):
    devices = got_ref.shape[0]
    rows = 256
    half = rows // 2
    piece = half // devices
    zero = jnp.zeros((64, rows), BF16)

    def key_weights(i):
        queries_t = jnp.concatenate([got_ref[i, 128:192, :], got_ref[i, 192:256, :]], axis=1)
        return (
            jnp.concatenate([queries_t, zero], axis=0),
            jnp.concatenate([zero, queries_t], axis=0),
        )

    def score(weights, scores, c, top):
        key_rows = got_ref[c, :128, :]
        for h in range(2):
            part = jnp.dot(key_rows, weights[h], preferred_element_type=F32)
            scores[c * rows + h * half : c * rows + (h + 1) * half, :] = part
            for b in range(half // 8):
                block = part[b * 8 : (b + 1) * 8]
                top = block if top is None else jnp.maximum(top, block)
        return top

    def weigh(scores, c, top, total):
        part = scores[c * rows : (c + 1) * rows, :]
        probs = jnp.exp2((part - top) * (0.125 * LOG2E)).astype(BF16)
        weighted = jnp.dot(
            values_t[:, c * rows : (c + 1) * rows], probs, preferred_element_type=F32
        )
        return weighted if total is None else total + weighted

    def keep(top):
        top_ref[...] = jnp.broadcast_to(jnp.max(top, axis=0, keepdims=True), top_ref.shape)

    for b in range(home_ref.shape[2] // 128):
        out_ref[:, half + b * piece : half + (b + 1) * piece, :] = home_ref[
            :, :, b * 128 : (b + 1) * 128
        ]
    for c in range(devices):
        values_t[:64, c * rows : c * rows + half] = got_ref[c, 256:320, :]
        values_t[:64, c * rows + half : (c + 1) * rows] = got_ref[c, 320:384, :]
    values_t[64:, :] = jnp.ones((values_t.shape[0] - 64, values_t.shape[1]), BF16)
    first_top = None
    first_weights = key_weights(0)
    for c in range(devices):
        first_top = score(first_weights, scores_a, c, first_top)
    keep(first_top)

    def phase(step, current, following):
        top = top_ref[:1, :]
        total = next_top = None
        if following is not None:
            weights = key_weights(step + 1)
        for c in range(devices):
            if following is not None:
                next_top = score(weights, following, c, next_top)
            total = weigh(current, c, top, total)
        if following is not None:
            keep(next_top)
        result = total[:64] / total[64:65]
        out_ref[step, 64:half, :] = result[:, half:].astype(BF16)
        if current is scores_a:
            even_ref[...] = result[:, :half]
        else:
            pair = jnp.concatenate([even_ref[...], result[:, :half]], axis=0).T
            at = pl.multiple_of(step // 2 * piece, piece)
            out_ref[:, pl.ds(at, piece), :] = pair.astype(BF16).reshape(devices, piece, 128)

    @pl.loop(0, devices - 1)
    def _(step):
        even = step % 2 == 0
        pl.when(even)(lambda: phase(step, scores_a, scores_b))
        pl.when(jnp.logical_not(even))(lambda: phase(step, scores_b, scores_a))

    phase(devices - 1, scores_a if devices % 2 else scores_b, None)


def attend(got, home):
    devices = got.shape[0]
    rows = 256
    everything = devices * rows
    in_vmem = pl.BlockSpec(memory_space=pltpu.VMEM)
    return pl.pallas_call(
        attend_kernel,
        out_shape=jax.ShapeDtypeStruct((devices, 192, 128), BF16),
        in_specs=[in_vmem, in_vmem],
        out_specs=in_vmem,
        scratch_shapes=[
            pltpu.VMEM((80, everything), BF16),
            pltpu.VMEM((everything, rows), F32),
            pltpu.VMEM((everything, rows), F32),
            pltpu.VMEM((8, rows), F32),
            pltpu.VMEM((64, rows // 2), F32),
        ],
        compiler_params=pltpu.CompilerParams(vmem_limit_bytes=24 << 20),
        name="attend",
    )(got, home)


def arrange_kernel(counts_ref, got_ref, rest_ref, rows_ref, packed_ref, home_at, rest_at):
    devices = got_ref.shape[0]
    piece = rows_ref.shape[1]
    quarter, half = 64, 128

    def visit(block, region, within, others):
        @pl.when(within == 0)
        def _():
            home_at[region] = block

        @pl.when(within > 0)
        def _():
            rest_at[others] = block

    walk_blocks(counts_ref, rows_ref.shape[0], visit)
    for c in range(devices):
        at = home_at[c]
        for b in range(packed_ref.shape[2] // 128):
            packed_ref[at, :, b * 128 : (b + 1) * 128] = got_ref[
                c, half + b * piece : half + (b + 1) * piece, :
            ]
    for k in range(rest_ref.shape[0] // piece):
        packed_ref[rest_at[k]] = rest_ref[k * piece : (k + 1) * piece, :]
    for p in range(devices // 2):
        lanes = slice(p * 128, (p + 1) * 128)
        one = got_ref[2 * p, :quarter, :].astype(F32)
        two = got_ref[2 * p + 1, :quarter, :].astype(F32)
        for odd in range(2):
            features = slice(odd * 64, (odd + 1) * 64)
            both = jnp.concatenate([one[:, features], two[:, features]], axis=1).astype(BF16)
            for c in range(devices // 2):
                rows_ref[home_at[2 * c + odd], :, lanes] = both[c * piece : (c + 1) * piece]
        others = jnp.concatenate(
            [got_ref[2 * p, quarter:half, :], got_ref[2 * p + 1, quarter:half, :]], axis=0
        )
        others = others.astype(F32).T.astype(BF16)
        for k in range(half // piece):
            rows_ref[rest_at[k], :, lanes] = others[k * piece : (k + 1) * piece]


def arrange(counts, got, rest, total, piece, d_model):
    devices = got.shape[0]
    in_vmem = pl.BlockSpec(memory_space=pltpu.VMEM)
    rows = jax.ShapeDtypeStruct((total, piece, d_model), BF16)
    return pl.pallas_call(
        arrange_kernel,
        out_shape=(rows, rows),
        in_specs=[pl.BlockSpec(memory_space=pltpu.SMEM)] + [in_vmem] * 2,
        out_specs=(in_vmem, in_vmem),
        scratch_shapes=[
            pltpu.SMEM((devices,), jnp.int32),
            pltpu.SMEM((total - devices,), jnp.int32),
        ],
        compiler_params=pltpu.CompilerParams(vmem_limit_bytes=16 << 20),
        name="arrange",
    )(counts, got, rest)


def body(patches, visible_count, visible_order, ln_gain, w_qkv, w_out):
    devices = lax.axis_size("ctx")
    blocks_dev = visible_order.shape[1]
    block_rows = patches.shape[0] // blocks_dev
    d_model = patches.shape[1]
    total_blocks = devices * blocks_dev // 4
    most = min(3 * blocks_dev // 4, total_blocks - devices + 1)
    piece = block_rows // devices
    gain = ln_gain.reshape(1, d_model)

    rest, home = select_blocks(visible_order, patches, most, block_rows, devices)
    received = lax.all_to_all(rest, "ctx", split_axis=0, concat_axis=0, tiled=True)
    received = received.reshape(devices * (most - 1), piece, d_model)
    packed, projected = project(
        visible_count, received, home, gain, w_qkv, total_blocks - devices
    )
    by_head = lax.all_to_all(projected, "ctx", split_axis=0, concat_axis=0, tiled=True)
    attended = attend(by_head, home)
    attended = lax.all_to_all(attended, "ctx", split_axis=0, concat_axis=0, tiled=True)
    attended, packed = arrange(visible_count, attended, packed, total_blocks, piece, d_model)
    mixed = packed.reshape(-1, d_model).astype(F32) + jnp.dot(
        attended.reshape(-1, d_model), w_out, preferred_element_type=F32
    )
    return mixed.astype(BF16)


def solution(mesh):
    return jax.shard_map(
        body,
        mesh=mesh,
        in_specs=(P(("dp", "ctx"), None), P("dp"), P(("dp", "ctx"), None), P(), P(), P()),
        out_specs=P(("dp", "ctx"), None),
        check_vma=False,
    )
```

```python
import jax
import jax.numpy as jnp
from jax import lax
from jax.experimental import pallas as pl
from jax.experimental.pallas import tpu as pltpu
from jax.sharding import PartitionSpec as P

HEADS = 16
EPSILON = 1e-05
LOG2E = 1.4426950408889634
STAGGER_NS = 19500
BF16 = jnp.bfloat16
F32 = jnp.float32


def select_kernel(order_ref, patches_ref, out_ref, sems):
    devices, rows, _ = out_ref.shape
    most = sems.shape[0]
    piece = rows // most
    copies = []
    for j in range(most):
        source = patches_ref.at[pl.ds(order_ref[0, j] * devices, devices)]
        target = out_ref.at[:, j * piece : (j + 1) * piece, :]
        copies.append(pltpu.make_async_copy(source, target, sems.at[j]))
    for copy in copies:
        copy.start()
    pl.when(lax.axis_index("dp") % 2 == 1)(lambda: pl.delay(STAGGER_NS))
    for copy in copies:
        copy.wait()


def select_blocks(order, patches, most, block_rows, devices):
    d_model = patches.shape[1]
    piece = block_rows // devices
    return pl.pallas_call(
        select_kernel,
        out_shape=jax.ShapeDtypeStruct((devices, most * piece, d_model), BF16),
        in_specs=[
            pl.BlockSpec(memory_space=pltpu.SMEM),
            pl.BlockSpec(memory_space=pltpu.HBM),
        ],
        out_specs=pl.BlockSpec(memory_space=pltpu.VMEM),
        scratch_shapes=[pltpu.SemaphoreType.DMA((most,))],
        compiler_params=pltpu.CompilerParams(vmem_limit_bytes=8 << 20),
        name="select_blocks",
    )(
        pltpu.with_memory_space_constraint(order, pltpu.HBM),
        pltpu.with_memory_space_constraint(
            patches.reshape(patches.shape[0] // piece, piece, d_model), pltpu.HBM
        ),
    )


def project_kernel(
    counts_ref, got_ref, gain_ref, weights_ref, packed_ref, out_ref, normed, slots
):
    total, most = slots.shape[0], got_ref.shape[0] // counts_ref.shape[0]
    piece = got_ref.shape[1]
    rows, d_model = normed.shape
    half = rows // 2

    def find(k, state):
        region, within = state
        slots[k] = region * most + within
        last = within + 1 >= counts_ref[region]
        return (
            jnp.where(last, jnp.minimum(region + 1, counts_ref.shape[0] - 1), region),
            jnp.where(last, 0, within + 1),
        )

    lax.fori_loop(0, total, find, (jnp.int32(0), jnp.int32(0)))
    for k in range(total):
        packed_ref[k * piece : (k + 1) * piece, :] = got_ref[slots[k]]
    values = packed_ref[...].astype(F32)
    mean = jnp.mean(values, axis=-1, keepdims=True)
    centered = values - mean
    variance = jnp.mean(centered * centered, axis=-1, keepdims=True)
    normed[...] = (centered * lax.rsqrt(variance + EPSILON) * gain_ref[...]).astype(BF16)

    width = 256
    rows_in = normed[...]

    def columns(group, start):
        lanes = pl.ds(pl.multiple_of(start + group * width, width), width)
        return jnp.dot(rows_in, weights_ref[:, lanes], preferred_element_type=F32)

    def group_step(group, _):
        queries_t = columns(group, 0).T
        keys = columns(group, d_model)
        values_t = columns(group, 2 * d_model).T
        for h in range(width // 64):
            lanes = slice(h * 64, (h + 1) * 64)
            head = group * (width // 64) + h
            out_ref[head, :half, :] = jnp.concatenate(
                [keys[:half, lanes], keys[half:, lanes]], axis=1
            ).astype(BF16)
            out_ref[head, half : half + 64, :] = queries_t[lanes, :half].astype(BF16)
            out_ref[head, half + 64 : rows, :] = queries_t[lanes, half:].astype(BF16)
            out_ref[head, rows : rows + 64, :] = values_t[lanes, :half].astype(BF16)
            out_ref[head, rows + 64 :, :] = values_t[lanes, half:].astype(BF16)
        return 0

    for group in range(d_model // width):
        group_step(group, 0)


def project(counts, got, gain, w_qkv, total):
    slot_count, piece, d_model = got.shape
    rows = total * piece
    in_vmem = pl.BlockSpec(memory_space=pltpu.VMEM)
    return pl.pallas_call(
        project_kernel,
        out_shape=(
            jax.ShapeDtypeStruct((rows, d_model), BF16),
            jax.ShapeDtypeStruct((HEADS, rows + 128, 128), BF16),
        ),
        in_specs=[pl.BlockSpec(memory_space=pltpu.SMEM), in_vmem, in_vmem, in_vmem],
        out_specs=(in_vmem, in_vmem),
        scratch_shapes=[
            pltpu.VMEM((rows, d_model), BF16),
            pltpu.SMEM((total,), jnp.int32),
        ],
        compiler_params=pltpu.CompilerParams(vmem_limit_bytes=24 << 20),
        name="project",
    )(counts, got, gain.reshape(1, d_model), w_qkv)


def attend_kernel(got_ref, out_ref, values_t, scores_a, scores_b, top_ref):
    devices = got_ref.shape[0]
    rows = out_ref.shape[2]
    half = rows // 2
    zero = jnp.zeros((64, rows), BF16)

    def key_weights(i):
        queries_t = jnp.concatenate([got_ref[i, 128:192, :], got_ref[i, 192:256, :]], axis=1)
        return (
            jnp.concatenate([queries_t, zero], axis=0),
            jnp.concatenate([zero, queries_t], axis=0),
        )

    def score(weights, scores, c, top):
        key_rows = got_ref[c, :128, :]
        for h in range(2):
            part = jnp.dot(key_rows, weights[h], preferred_element_type=F32)
            scores[c * rows + h * half : c * rows + (h + 1) * half, :] = part
            for b in range(half // 8):
                block = part[b * 8 : (b + 1) * 8]
                top = block if top is None else jnp.maximum(top, block)
        return top

    def weigh(scores, c, top, total):
        part = scores[c * rows : (c + 1) * rows, :]
        probs = jnp.exp2((part - top) * (0.125 * LOG2E)).astype(BF16)
        weighted = jnp.dot(
            values_t[:, c * rows : (c + 1) * rows], probs, preferred_element_type=F32
        )
        return weighted if total is None else total + weighted

    def keep(top):
        top_ref[...] = jnp.broadcast_to(jnp.max(top, axis=0, keepdims=True), top_ref.shape)

    for c in range(devices):
        values_t[:64, c * rows : c * rows + half] = got_ref[c, 256:320, :]
        values_t[:64, c * rows + half : (c + 1) * rows] = got_ref[c, 320:384, :]
    values_t[64:, :] = jnp.ones((values_t.shape[0] - 64, values_t.shape[1]), BF16)
    first_top = None
    first_weights = key_weights(0)
    for c in range(devices):
        first_top = score(first_weights, scores_a, c, first_top)
    keep(first_top)

    def phase(step, current, following):
        top = top_ref[:1, :]
        total = next_top = None
        if following is not None:
            weights = key_weights(step + 1)
        for c in range(devices):
            if following is not None:
                next_top = score(weights, following, c, next_top)
            total = weigh(current, c, top, total)
        if following is not None:
            keep(next_top)
        out_ref[step] = (total[:64] / total[64:65]).astype(BF16)

    @pl.loop(0, devices - 1)
    def _(step):
        even = step % 2 == 0
        pl.when(even)(lambda: phase(step, scores_a, scores_b))
        pl.when(jnp.logical_not(even))(lambda: phase(step, scores_b, scores_a))

    phase(devices - 1, scores_a if devices % 2 else scores_b, None)


def attend(got):
    devices, packed_rows, lanes = got.shape
    rows = 256
    everything = devices * rows
    return pl.pallas_call(
        attend_kernel,
        out_shape=jax.ShapeDtypeStruct((devices, 64, rows), BF16),
        in_specs=[pl.BlockSpec(memory_space=pltpu.VMEM)],
        out_specs=pl.BlockSpec(memory_space=pltpu.VMEM),
        scratch_shapes=[
            pltpu.VMEM((80, everything), BF16),
            pltpu.VMEM((everything, rows), F32),
            pltpu.VMEM((everything, rows), F32),
            pltpu.VMEM((8, rows), F32),
        ],
        compiler_params=pltpu.CompilerParams(vmem_limit_bytes=24 << 20),
        name="attend",
    )(got)


def body(patches, visible_count, visible_order, ln_gain, w_qkv, w_out):
    devices = lax.axis_size("ctx")
    blocks_dev = visible_order.shape[1]
    block_rows = patches.shape[0] // blocks_dev
    d_model = patches.shape[1]
    total_blocks = devices * blocks_dev // 4
    most = min(3 * blocks_dev // 4, total_blocks - devices + 1)
    piece = block_rows // devices

    chosen = select_blocks(visible_order, patches, most, block_rows, devices)
    received = lax.all_to_all(chosen, "ctx", split_axis=0, concat_axis=0, tiled=True)
    received = received.reshape(devices * most, piece, d_model)
    packed, projected = project(visible_count, received, ln_gain, w_qkv, total_blocks)
    by_head = lax.all_to_all(projected, "ctx", split_axis=0, concat_axis=0, tiled=True)
    attended = attend(by_head)
    attended = lax.all_to_all(attended, "ctx", split_axis=0, concat_axis=0, tiled=True)
    attended = attended.reshape(d_model, total_blocks * piece)
    mixed = packed.astype(F32) + lax.dot_general(
        attended, w_out, (((0,), (0,)), ((), ())), preferred_element_type=F32
    )
    return mixed.astype(BF16)


def solution(mesh):
    return jax.shard_map(
        body,
        mesh=mesh,
        in_specs=(P(("dp", "ctx"), None), P("dp"), P(("dp", "ctx"), None), P(), P(), P()),
        out_specs=P(("dp", "ctx"), None),
        check_vma=False,
    )
```

```python
import jax
import jax.numpy as jnp
from jax import lax
from jax.experimental import pallas as pl
from jax.experimental.pallas import tpu as pltpu
from jax.sharding import PartitionSpec as P

HEADS = 16
EPSILON = 1e-05
LOG2E = 1.4426950408889634
STAGGER_NS = 15000
BF16 = jnp.bfloat16
F32 = jnp.float32


def select_kernel(order_ref, patches_ref, out_ref, sems):
    devices, rows, _ = out_ref.shape
    most = sems.shape[0]
    piece = rows // most
    copies = []
    for j in range(most):
        source = patches_ref.at[pl.ds(order_ref[0, j] * devices, devices)]
        target = out_ref.at[:, j * piece : (j + 1) * piece, :]
        copies.append(pltpu.make_async_copy(source, target, sems.at[j]))
    for copy in copies:
        copy.start()
    pl.when(lax.axis_index("dp") % 2 == 0)(lambda: pl.delay(STAGGER_NS))
    for copy in copies:
        copy.wait()


def select_blocks(order, patches, most, block_rows, devices):
    d_model = patches.shape[1]
    piece = block_rows // devices
    return pl.pallas_call(
        select_kernel,
        out_shape=jax.ShapeDtypeStruct((devices, most * piece, d_model), BF16),
        in_specs=[
            pl.BlockSpec(memory_space=pltpu.SMEM),
            pl.BlockSpec(memory_space=pltpu.HBM),
        ],
        out_specs=pl.BlockSpec(memory_space=pltpu.VMEM),
        scratch_shapes=[pltpu.SemaphoreType.DMA((most,))],
        compiler_params=pltpu.CompilerParams(vmem_limit_bytes=8 << 20),
        name="select_blocks",
    )(
        pltpu.with_memory_space_constraint(order, pltpu.HBM),
        pltpu.with_memory_space_constraint(
            patches.reshape(patches.shape[0] // piece, piece, d_model), pltpu.HBM
        ),
    )


def project_kernel(
    counts_ref, got_ref, gain_ref, weights_ref, packed_ref, out_ref, normed, slots
):
    total, most = slots.shape[0], got_ref.shape[0] // counts_ref.shape[0]
    piece = got_ref.shape[1]
    rows, d_model = normed.shape
    half = rows // 2

    def find(k, state):
        region, within = state
        slots[k] = region * most + within
        last = within + 1 >= counts_ref[region]
        return (
            jnp.where(last, jnp.minimum(region + 1, counts_ref.shape[0] - 1), region),
            jnp.where(last, 0, within + 1),
        )

    lax.fori_loop(0, total, find, (jnp.int32(0), jnp.int32(0)))
    for k in range(total):
        packed_ref[k * piece : (k + 1) * piece, :] = got_ref[slots[k]]
    values = packed_ref[...].astype(F32)
    mean = jnp.mean(values, axis=-1, keepdims=True)
    centered = values - mean
    variance = jnp.mean(centered * centered, axis=-1, keepdims=True)
    normed[...] = (centered * lax.rsqrt(variance + EPSILON) * gain_ref[...]).astype(BF16)

    width = 256
    rows_in = normed[...]

    def columns(group, start):
        lanes = pl.ds(pl.multiple_of(start + group * width, width), width)
        return jnp.dot(rows_in, weights_ref[:, lanes], preferred_element_type=F32)

    def group_step(group, _):
        queries_t = columns(group, 0).T
        keys = columns(group, d_model)
        values_t = columns(group, 2 * d_model).T
        for h in range(width // 64):
            lanes = slice(h * 64, (h + 1) * 64)
            head = group * (width // 64) + h
            out_ref[head, :half, :] = jnp.concatenate(
                [keys[:half, lanes], keys[half:, lanes]], axis=1
            ).astype(BF16)
            out_ref[head, half : half + 64, :] = queries_t[lanes, :half].astype(BF16)
            out_ref[head, half + 64 : rows, :] = queries_t[lanes, half:].astype(BF16)
            out_ref[head, rows : rows + 64, :] = values_t[lanes, :half].astype(BF16)
            out_ref[head, rows + 64 :, :] = values_t[lanes, half:].astype(BF16)
        return 0

    for group in range(d_model // width):
        group_step(group, 0)


def project(counts, got, gain, w_qkv, total):
    slot_count, piece, d_model = got.shape
    rows = total * piece
    in_vmem = pl.BlockSpec(memory_space=pltpu.VMEM)
    return pl.pallas_call(
        project_kernel,
        out_shape=(
            jax.ShapeDtypeStruct((rows, d_model), BF16),
            jax.ShapeDtypeStruct((HEADS, rows + 128, 128), BF16),
        ),
        in_specs=[pl.BlockSpec(memory_space=pltpu.SMEM), in_vmem, in_vmem, in_vmem],
        out_specs=(in_vmem, in_vmem),
        scratch_shapes=[
            pltpu.VMEM((rows, d_model), BF16),
            pltpu.SMEM((total,), jnp.int32),
        ],
        compiler_params=pltpu.CompilerParams(vmem_limit_bytes=24 << 20),
        name="project",
    )(counts, got, gain.reshape(1, d_model), w_qkv)


def attend_kernel(got_ref, out_ref, values_t, scores_a, scores_b, top_ref):
    devices = got_ref.shape[0]
    rows = out_ref.shape[2]
    half = rows // 2
    zero = jnp.zeros((64, rows), BF16)

    def key_weights(i):
        queries_t = jnp.concatenate([got_ref[i, 128:192, :], got_ref[i, 192:256, :]], axis=1)
        return (
            jnp.concatenate([queries_t, zero], axis=0),
            jnp.concatenate([zero, queries_t], axis=0),
        )

    def score(weights, scores, c, top):
        key_rows = got_ref[c, :128, :]
        for h in range(2):
            part = jnp.dot(key_rows, weights[h], preferred_element_type=F32)
            scores[c * rows + h * half : c * rows + (h + 1) * half, :] = part
            for b in range(half // 8):
                block = part[b * 8 : (b + 1) * 8]
                top = block if top is None else jnp.maximum(top, block)
        return top

    def weigh(scores, c, top, total):
        part = scores[c * rows : (c + 1) * rows, :]
        probs = jnp.exp2((part - top) * (0.125 * LOG2E)).astype(BF16)
        weighted = jnp.dot(
            values_t[:, c * rows : (c + 1) * rows], probs, preferred_element_type=F32
        )
        return weighted if total is None else total + weighted

    def keep(top):
        top_ref[...] = jnp.broadcast_to(jnp.max(top, axis=0, keepdims=True), top_ref.shape)

    for c in range(devices):
        values_t[:64, c * rows : c * rows + half] = got_ref[c, 256:320, :]
        values_t[:64, c * rows + half : (c + 1) * rows] = got_ref[c, 320:384, :]
    values_t[64:, :] = jnp.ones((values_t.shape[0] - 64, values_t.shape[1]), BF16)
    first_top = None
    first_weights = key_weights(0)
    for c in range(devices):
        first_top = score(first_weights, scores_a, c, first_top)
    keep(first_top)

    def phase(step, current, following):
        top = top_ref[:1, :]
        total = next_top = None
        if following is not None:
            weights = key_weights(step + 1)
        for c in range(devices):
            if following is not None:
                next_top = score(weights, following, c, next_top)
            total = weigh(current, c, top, total)
        if following is not None:
            keep(next_top)
        out_ref[step] = (total[:64] / total[64:65]).astype(BF16)

    @pl.loop(0, devices - 1)
    def _(step):
        even = step % 2 == 0
        pl.when(even)(lambda: phase(step, scores_a, scores_b))
        pl.when(jnp.logical_not(even))(lambda: phase(step, scores_b, scores_a))

    phase(devices - 1, scores_a if devices % 2 else scores_b, None)


def attend(got):
    devices, packed_rows, lanes = got.shape
    rows = 256
    everything = devices * rows
    return pl.pallas_call(
        attend_kernel,
        out_shape=jax.ShapeDtypeStruct((devices, 64, rows), BF16),
        in_specs=[pl.BlockSpec(memory_space=pltpu.VMEM)],
        out_specs=pl.BlockSpec(memory_space=pltpu.VMEM),
        scratch_shapes=[
            pltpu.VMEM((80, everything), BF16),
            pltpu.VMEM((everything, rows), F32),
            pltpu.VMEM((everything, rows), F32),
            pltpu.VMEM((8, rows), F32),
        ],
        compiler_params=pltpu.CompilerParams(vmem_limit_bytes=24 << 20),
        name="attend",
    )(got)


def body(patches, visible_count, visible_order, ln_gain, w_qkv, w_out):
    devices = lax.axis_size("ctx")
    blocks_dev = visible_order.shape[1]
    block_rows = patches.shape[0] // blocks_dev
    d_model = patches.shape[1]
    total_blocks = devices * blocks_dev // 4
    most = min(3 * blocks_dev // 4, total_blocks - devices + 1)
    piece = block_rows // devices

    chosen = select_blocks(visible_order, patches, most, block_rows, devices)
    received = lax.all_to_all(chosen, "ctx", split_axis=0, concat_axis=0, tiled=True)
    received = received.reshape(devices * most, piece, d_model)
    packed, projected = project(visible_count, received, ln_gain, w_qkv, total_blocks)
    by_head = lax.all_to_all(projected, "ctx", split_axis=0, concat_axis=0, tiled=True)
    attended = attend(by_head)
    attended = lax.all_to_all(attended, "ctx", split_axis=0, concat_axis=0, tiled=True)
    attended = attended.reshape(d_model, total_blocks * piece)
    mixed = packed.astype(F32) + lax.dot_general(
        attended, w_out, (((0,), (0,)), ((), ())), preferred_element_type=F32
    )
    return mixed.astype(BF16)


def solution(mesh):
    return jax.shard_map(
        body,
        mesh=mesh,
        in_specs=(P(("dp", "ctx"), None), P("dp"), P(("dp", "ctx"), None), P(), P(), P()),
        out_specs=P(("dp", "ctx"), None),
        check_vma=False,
    )
```
